32 devices in a mesh: dp: 8 (over z, y), tensor: 4 (over x, core).
Axes of the slice: x: 2, y: 2, z: 4, core: 2. Of those that a mesh axis runs over, the one named last changes fastest.
Arguments:
- gate_pre: bfloat16 [512, 16384], P('dp', 'tensor'), may hold values from -6 to 6
- up_pre: bfloat16 [512, 16384], P('dp', 'tensor'), may hold values from -6 to 6
- cotangent: bfloat16 [512, 4096], P(('dp', 'tensor')), may hold values from -6 to 6
- down_blocks: bfloat16 [4, 256, 4096], P('tensor'), may hold values from -0.1875 to 0.1875
- live_blocks: int32 [4, 256], P('tensor'), may hold values from 0 to 4095, as said below
Outputs:
- layer_out: bfloat16 [512, 4096], P(('dp', 'tensor'))
- gate_grad: bfloat16 [512, 16384], P('dp', 'tensor')
- up_grad: bfloat16 [512, 16384], P('dp', 'tensor')
- weight_grad: float32 [4, 256, 4096], P('tensor', 'dp')
The draws below stay inside these ranges and needn't reach their ends.
Inputs may be any that keep to these rules, and one draw needn't show every extreme that they name: `live_blocks`: in each row, the 256 numbers are distinct; block 0 and the last block number are live in every shard.
All inputs are finite; a program needn't handle non-finite values.
Results may differ from the reference program's by a relative error of at most 0.013.
Values may be sent and summed in bfloat16 or wider, within the bound.
A program may use at most 64 MiB of HBM per device.

```python
import jax
import jax.numpy as jnp
from jax import lax

D = 4096
FF = 16384
BLOCK = 64
KEEP = 16
TOK_DEV = 16
LIVE = 256
TOKENS = 512
N_DP = 8
N_TENSOR = 4


def live_table(key):
    grid = FF // N_TENSOR // BLOCK * (D // BLOCK)

    def one_shard(shard):
        inner = jax.random.permutation(jax.random.fold_in(key, shard), grid - 2)[:LIVE - 2] + 1
        ends = jnp.array([0, grid - 1], jnp.int32)
        return jnp.concatenate([ends, inner.astype(jnp.int32)])
    return jax.vmap(one_shard)(jnp.arange(N_TENSOR))


def draw_live_blocks(key, part):
    return live_table(key)


def block_scale(own_key, shape, cuts, smallest, top_value):
    level = 1.0
    for axis_at, blocks in cuts:
        draws = jax.random.uniform(jax.random.fold_in(jax.random.fold_in(own_key, 6), axis_at), (blocks,), jnp.float32, smallest / len(cuts), top_value / len(cuts))
        level = level * jnp.repeat(jnp.exp(draws), shape[axis_at] // blocks).reshape((-1,) + (1,) * (len(shape) - 1 - axis_at))
    return level


def gaussian(stream_key, dims, spread, limit, shards=(), held_as=jnp.bfloat16):
    factor_of = block_scale(stream_key, dims, shards, -0.22, 0.18) if shards else 1.0
    result = jax.random.normal(stream_key, dims, jnp.float32) * spread * factor_of
    return jnp.minimum(jnp.maximum(result, -limit), limit).astype(held_as)


def setup_inputs(seed: int = 0) -> dict:
    key_list = jax.random.split(jax.random.key(seed), 6)
    return {
        "gate_pre": gaussian(key_list[0], (TOKENS, FF), 1.0, 6.0, ((0, 8), (1, 4))),
        "up_pre": gaussian(key_list[1], (TOKENS, FF), 1.0, 6.0, ((0, 8), (1, 4))),
        "cotangent": gaussian(key_list[2], (TOKENS, D), 1.0, 6.0, ((0, 32),)),
        "down_blocks": gaussian(key_list[3], (N_TENSOR, LIVE, BLOCK * BLOCK), (FF // KEEP) ** -0.5, 0.1875, ((0, 4),)),
        "live_blocks": draw_live_blocks(jax.random.fold_in(key_list[5], 71), 0),
    }


def reference(gate_pre, up_pre, cotangent, down_blocks, live_blocks):
    rows = TOK_DEV * N_TENSOR
    ff_dev = FF // N_TENSOR
    hid_count = ff_dev // BLOCK
    col_count = D // BLOCK
    gates = gate_pre.reshape(N_DP, rows, FF)
    ups = up_pre.reshape(N_DP, rows, FF)
    cots = cotangent.reshape(N_DP, rows, D)
    weights = down_blocks.astype(jnp.float32).reshape(N_TENSOR, LIVE, BLOCK, BLOCK)
    hid_ids = (live_blocks // col_count).astype(jnp.int32)
    col_ids = (live_blocks % col_count).astype(jnp.int32)

    def replica(carry, inputs):
        gate_r, up_r, cot_r = inputs
        gate32 = gate_r.astype(jnp.float32)
        up32 = up_r.astype(jnp.float32)
        sig = jax.nn.sigmoid(gate32)
        silu_g = gate32 * sig
        hidden = (silu_g * up32).astype(jnp.bfloat16)
        cot_blocks = cot_r.astype(jnp.float32).reshape(rows, col_count, BLOCK)
        out_sum = jnp.zeros((rows, D), jnp.float32)
        dh_parts = []
        new_carry = []
        for shard in range(N_TENSOR):
            h_shard = hidden[:, shard * ff_dev:(shard + 1) * ff_dev].astype(jnp.float32)
            hsel = h_shard.reshape(rows, hid_count, BLOCK)[:, hid_ids[shard], :]
            dysel = cot_blocks[:, col_ids[shard], :]
            prod = jnp.einsum('tlk,lkj->tlj', hsel, weights[shard])
            part = jnp.zeros((rows, col_count, BLOCK), jnp.float32).at[:, col_ids[shard], :].add(prod)
            part = lax.optimization_barrier(part.reshape(rows, D).astype(jnp.bfloat16))
            out_sum = out_sum + part.astype(jnp.float32)
            dh_blk = jnp.einsum('tlj,lkj->tlk', dysel, weights[shard])
            dh = jnp.zeros((rows, hid_count, BLOCK), jnp.float32).at[:, hid_ids[shard], :].add(dh_blk)
            dh_parts.append(dh.reshape(rows, ff_dev))
            grad = jnp.einsum('tlk,tlj->lkj', hsel, dysel).reshape(LIVE, BLOCK * BLOCK)
            new_carry.append(carry[shard] + grad)
        dh_all = jnp.concatenate(dh_parts, axis=1)
        gate_g = (dh_all * up32 * sig * (1.0 + gate32 * (1.0 - sig))).astype(jnp.bfloat16)
        up_g = (dh_all * silu_g).astype(jnp.bfloat16)
        return (jnp.stack(new_carry), (out_sum.astype(jnp.bfloat16), gate_g, up_g))
    start = jnp.zeros((N_TENSOR, LIVE, BLOCK * BLOCK), jnp.float32)
    grads, outs = lax.scan(replica, start, (gates, ups, cots))
    layer_out = outs[0].reshape(TOKENS, D)
    gate_grad = outs[1].reshape(TOKENS, FF)
    up_grad = outs[2].reshape(TOKENS, FF)
    weight_grad = grads / jnp.sqrt(jnp.float32(TOKENS))
    return (layer_out, gate_grad, up_grad, weight_grad)
```

```python
import functools
import math

import jax
import jax.numpy as jnp
from jax import lax
from jax.experimental import pallas as pl
from jax.experimental.pallas import tpu as pltpu
from jax.sharding import PartitionSpec as P

D = 4096
BLOCK = 64
COLS = D // BLOCK
LANES = 2 * BLOCK


def plain(gate_pre, up_pre, cotangent, down_blocks, live_blocks):
    rows, ff_dev = gate_pre.shape
    live = live_blocks.shape[1]
    hid_count = ff_dev // BLOCK
    col_count = D // BLOCK
    block_ids = live_blocks[0]
    hid_ids = block_ids // col_count
    col_ids = block_ids % col_count
    weights = down_blocks[0].reshape(live, BLOCK, BLOCK)
    col_onehot = (col_ids[:, None] == jnp.arange(col_count)[None, :]).astype(jnp.float32)
    hid_onehot = (hid_ids[:, None] == jnp.arange(hid_count)[None, :]).astype(jnp.float32)
    gate32 = gate_pre.astype(jnp.float32)
    up32 = up_pre.astype(jnp.float32)
    sig = jax.nn.sigmoid(gate32)
    silu_g = gate32 * sig
    hidden = (silu_g * up32).astype(jnp.bfloat16)
    hsel = hidden.T.reshape(hid_count, BLOCK, rows)[hid_ids]
    prod = jnp.einsum("lkt,lkj->ljt", hsel, weights, preferred_element_type=jnp.float32)
    spread = jnp.einsum("ljt,lc->cjt", prod, col_onehot).reshape(D, rows).T
    layer_out = lax.psum_scatter(
        spread.astype(jnp.bfloat16), "tensor", scatter_dimension=0, tiled=True
    )
    cot_full = lax.all_gather(cotangent, "tensor", axis=0, tiled=True)
    dysel = cot_full.T.reshape(col_count, BLOCK, rows)[col_ids]
    dh_blk = jnp.einsum("ljt,lkj->lkt", dysel, weights, preferred_element_type=jnp.float32)
    hidden_grad = jnp.einsum("lkt,lh->hkt", dh_blk, hid_onehot).reshape(ff_dev, rows).T
    gate_grad = (hidden_grad * up32 * sig * (1.0 + gate32 * (1.0 - sig))).astype(jnp.bfloat16)
    up_grad = (hidden_grad * silu_g).astype(jnp.bfloat16)
    scale = 1.0 / math.sqrt(rows * lax.axis_size("dp"))
    term = jnp.einsum("lkt,ljt->lkj", hsel, dysel, preferred_element_type=jnp.float32)
    term = term.reshape(live, BLOCK * BLOCK) * scale
    weight_grad = lax.psum_scatter(term, "dp", scatter_dimension=0, tiled=True)
    return (layer_out, gate_grad, up_grad, weight_grad[None])


def pair_at(ids_ref, p, half):
    a = (p // half) * (2 * half) + p % half
    first, second = ids_ref[0, a], ids_ref[0, a + half]
    return first // COLS, second // COLS, first % COLS, second % COLS


def lane_low(shape):
    return lax.broadcasted_iota(jnp.int32, shape, 1) < BLOCK


def flip_in(x32, out_ref, c):
    both = jnp.concatenate([x32, x32], axis=0).T.astype(jnp.bfloat16)
    out_ref[2 * c] = both[:BLOCK]
    out_ref[2 * c + 1] = both[BLOCK:]


def flip_out(acc_ref, c):
    both = jnp.concatenate([acc_ref[2 * c], acc_ref[2 * c + 1]], axis=0).T
    return both[:BLOCK] + both[BLOCK:]


def chunk_of(c):
    return pl.ds(pl.multiple_of(c * LANES, LANES), LANES)


def term_kernel(half, scale, ids_ref, gate_ref, up_ref, cot_ref, term_ref, ht_ref, ct_ref):
    def turn(c, _):
        at = chunk_of(c)
        gate = gate_ref[:, at].astype(jnp.float32)
        hidden = gate * jax.nn.sigmoid(gate) * up_ref[:, at].astype(jnp.float32)
        flip_in(hidden.astype(jnp.bfloat16).astype(jnp.float32), ht_ref, c)
        flip_in(cot_ref[:, at].astype(jnp.float32), ct_ref, c)
        return 0

    lax.fori_loop(0, gate_ref.shape[1] // LANES, turn, 0, unroll=4)
    low = lane_low((BLOCK, LANES))

    def pair(p, _):
        ha, hb, ca, cb = pair_at(ids_ref, p, half)
        h = jnp.concatenate([ht_ref[ha], ht_ref[hb]], axis=0)
        c = jnp.concatenate([ct_ref[ca], ct_ref[cb]], axis=0)
        r = lax.dot_general(h, c, (((1,), (1,)), ((), ())), preferred_element_type=jnp.float32)
        term_ref[p] = (jnp.where(low, r[:BLOCK], r[BLOCK:]) * (0.5 * scale)).astype(jnp.bfloat16)
        return 0

    lax.fori_loop(0, term_ref.shape[0], pair, 0, unroll=8)


def product_kernel(half, ids_ref, gate_ref, up_ref, ht_ref, ct_ref, w_ref, part_ref, gg_ref, ug_ref, out_acc, dh_acc):
    out_acc[...] = jnp.zeros_like(out_acc)
    dh_acc[...] = jnp.zeros_like(dh_acc)
    low = lane_low((BLOCK, LANES))
    keep_a = low.astype(jnp.float32).astype(jnp.bfloat16)
    keep_b = (1.0 - low.astype(jnp.float32)).astype(jnp.bfloat16)
    group = 4

    def pairs(g, _):
        done = []
        for i in range(group):
            p = g * group + i
            ha, hb, ca, cb = pair_at(ids_ref, p, half)
            w = w_ref[p]
            h = ht_ref[ha] * keep_a + ht_ref[hb] * keep_b
            r1 = lax.dot_general(w, h, (((0,), (0,)), ((), ())), preferred_element_type=jnp.float32)
            c = jnp.concatenate([ct_ref[ca] * keep_a, ct_ref[cb] * keep_b], axis=0)
            r2 = jnp.dot(w, c, preferred_element_type=jnp.float32)
            done.append((ha, hb, ca, cb, r1, r2))
        for ha, hb, ca, cb, r1, r2 in done:
            out_acc[ca] += jnp.where(low, r1[:BLOCK], 0.0)
            out_acc[cb] += jnp.where(low, 0.0, r1[BLOCK:])
            dh_acc[ha] += jnp.where(low, r2, 0.0)
            dh_acc[hb] += jnp.where(low, 0.0, r2)
        return 0

    lax.fori_loop(0, w_ref.shape[0] // group, pairs, 0)

    def finish(c, _):
        at = chunk_of(c)
        part_ref[:, at] = flip_out(out_acc, c).astype(jnp.bfloat16)
        dh = flip_out(dh_acc, c)
        gate = gate_ref[:, at].astype(jnp.float32)
        up = up_ref[:, at].astype(jnp.float32)
        sig = jax.nn.sigmoid(gate)
        gg_ref[:, at] = (dh * up * sig * (1.0 + gate * (1.0 - sig))).astype(jnp.bfloat16)
        ug_ref[:, at] = (dh * (gate * sig)).astype(jnp.bfloat16)
        return 0

    lax.fori_loop(0, gate_ref.shape[1] // LANES, finish, 0, unroll=4)


def vmem(n):
    return [pl.BlockSpec(memory_space=pltpu.VMEM)] * n


SMEM_SPEC = pl.BlockSpec(memory_space=pltpu.SMEM)


def on_device(gate_pre, up_pre, cotangent, down_blocks, live_blocks):
    rows, ff_dev = gate_pre.shape
    live = live_blocks.shape[1]
    n_dp, n_tensor = lax.axis_size("dp"), lax.axis_size("tensor")
    if rows != BLOCK or ff_dev != D or live % (2 * n_dp) or live % 8:
        return plain(gate_pre, up_pre, cotangent, down_blocks, live_blocks)
    half = live // n_dp // 2
    scale = 1.0 / math.sqrt(rows * n_dp)
    cot_full = lax.all_gather(cotangent, "tensor", axis=0, tiled=True)
    stack = jax.ShapeDtypeStruct((COLS, BLOCK, LANES), jnp.bfloat16)
    term, ht, ct = pl.pallas_call(
        functools.partial(term_kernel, half, scale),
        out_shape=(jax.ShapeDtypeStruct((live // 2, BLOCK, LANES), jnp.bfloat16), stack, stack),
        in_specs=[SMEM_SPEC] + vmem(3),
        out_specs=tuple(vmem(3)),
        cost_estimate=pl.CostEstimate(flops=10**9, bytes_accessed=2**23, transcendentals=2**18),
    )(live_blocks, gate_pre, up_pre, cot_full)
    summed = lax.psum_scatter(term, "dp", scatter_dimension=0, tiled=True)
    paired = down_blocks[0].reshape(n_dp, 2, half, BLOCK, BLOCK).transpose(0, 2, 3, 1, 4)
    paired = paired.reshape(live // 2, BLOCK, LANES)
    whole = jax.ShapeDtypeStruct((rows, D), jnp.bfloat16)
    part, gate_grad, up_grad = pl.pallas_call(
        functools.partial(product_kernel, half),
        out_shape=(whole, whole, whole),
        in_specs=[SMEM_SPEC] + vmem(5),
        out_specs=tuple(vmem(3)),
        scratch_shapes=[pltpu.VMEM((COLS, BLOCK, LANES), jnp.float32)] * 2,
        cost_estimate=pl.CostEstimate(flops=10**9, bytes_accessed=2**24, transcendentals=2**18),
    )(live_blocks, gate_pre, up_pre, ht, ct, paired)
    shares = lax.all_to_all(part.reshape(n_tensor, rows // n_tensor, D), "tensor", 0, 0)
    layer_out = jnp.sum(shares.astype(jnp.float32), axis=0).astype(jnp.bfloat16)
    grad = summed.astype(jnp.float32).reshape(half, BLOCK, 2, BLOCK).transpose(2, 0, 1, 3)
    return (layer_out, gate_grad, up_grad, grad.reshape(1, 2 * half, BLOCK * BLOCK))


def solution(mesh):
    in_specs = (
        P("dp", "tensor"),
        P("dp", "tensor"),
        P(("dp", "tensor"), None),
        P("tensor", None, None),
        P("tensor", None),
    )
    out_specs = (
        P(("dp", "tensor"), None),
        P("dp", "tensor"),
        P("dp", "tensor"),
        P("tensor", "dp", None),
    )
    return jax.shard_map(
        on_device, mesh=mesh, in_specs=in_specs, out_specs=out_specs, check_vma=False
    )
```
